32 devices in a mesh: group: 2 (over y), wide: 8 (over z, x), narrow: 2 (over core).
Axes of the slice: x: 2, y: 2, z: 4, core: 2. Of those that a mesh axis runs over, the one named last changes fastest.
Arguments:
- hidden_in: bfloat16 [16, 16384], P(('group', 'wide'), 'narrow'), parts along dimension 0, may hold values from -60 to 60
- norm_gain: float32 [16384], P('narrow'), may hold values from 0.1 to 1.9
- qkv_weight: bfloat16 [16384, 9216], P('narrow', 'wide'), may hold values from -0.046875 to 0.046875
- out_weight: bfloat16 [8192, 16384], P('narrow', 'wide'), may hold values from -0.25 to 0.25
- cache_keys: bfloat16 [16, 256, 512], P(('group', 'wide'), None, 'narrow'), parts along dimension 0, may hold values from -500 to 500
- cache_values: bfloat16 [16, 256, 512], P(('group', 'wide'), None, 'narrow'), parts along dimension 0, may hold values from -6 to 6
- cache_lengths: int32 [16], P(('group', 'wide')), parts along dimension 0, may hold values from 4 to 256, as said below
Outputs:
- layer_out: float32 [16, 16384], P(('group', 'wide'), 'narrow'), parts along dimension 0
The draws below stay inside these ranges and needn't reach their ends.
There are 2 independent parts, one for each index of `group`. The reference program is written for one: setup_inputs(seed, part) draws one part's arguments, and reference() takes and returns one part's arrays. A program takes and returns all parts, laid end to end along the dimension named above; an argument that names none is the same for every part. Nothing has to cross between parts.
Inputs may be any that keep to these rules, and one draw needn't show every extreme that they name: Some row's length is exactly 256 in every draw; row r's cached positions are 0 to cache_lengths[r] - 1 and its new token stands at position cache_lengths[r].
All inputs are finite; a program needn't handle non-finite values.
Results may differ from the reference program's by a relative error of at most 0.0058.
Values may be sent and summed in bfloat16 or wider, within the bound.
No kernel may reach another device: no remote copies, remote signals or barrier semaphores. Data moves between devices by JAX's collectives and lax.ppermute only.
A program may use at most 64 MiB of HBM per device.

```python
import jax
import jax.numpy as jnp
from jax import lax

D = 16384
QH = 64
KVH = 4
HD = 128
CTX = 256
GQ = 16
COLS = 9216
ROWS = 8


def draw_cache_lengths(key, part):
    first_key, second_key = jax.random.split(jax.random.fold_in(key, 11))
    lengths = jax.random.randint(first_key, (ROWS,), 4, CTX + 1)
    longest = jax.random.randint(second_key, (), 0, ROWS)
    return jnp.where(jnp.arange(ROWS) == longest, CTX, lengths).astype(jnp.int32)


def draw_cache_keys(key, part):
    first_key = jax.random.fold_in(jax.random.fold_in(key, 23), 0)
    base = jnp.clip(jax.random.normal(first_key, (ROWS, CTX, KVH * HD), jnp.float32), -6.0, 6.0) * 2.5
    return base.astype(jnp.bfloat16)


def draw_hidden_in(key, part):
    first_key, second_key = jax.random.split(jax.random.fold_in(key, 37))
    spot = jnp.arange(D, dtype=jnp.float32) / (D - 1.0)
    column_scale = jnp.exp(jnp.log(0.3) + spot * jnp.log(10.0))
    values = jnp.clip(jax.random.normal(first_key, (ROWS, D), jnp.float32), -6.0, 6.0)
    row_scale = jnp.exp(jax.random.uniform(second_key, (ROWS, 1), jnp.float32, jnp.log(0.5), jnp.log(2.0)))
    return (values * column_scale[None, :] * row_scale).astype(jnp.bfloat16)


def block_scale(own_key, dims, pieces, smallest, high):
    def one(axis_at, shards_of):
        steps = jax.random.uniform(jax.random.fold_in(jax.random.fold_in(own_key, 6), axis_at), (shards_of,), jnp.float32, smallest / len(pieces), high / len(pieces))
        return jnp.repeat(jnp.exp(steps), dims[axis_at] // shards_of).reshape((-1,) + (1,) * (len(dims) - axis_at - 1))

    gain = one(*pieces[0])
    for cut in pieces[1:]:
        gain = gain * one(*cut)
    return gain


def normal_values(rng, dims, scale, most, cuts=(), kind=jnp.bfloat16):
    level = block_scale(rng, dims, cuts, -0.22, 0.18) if cuts else 1.0
    values = jax.random.normal(rng, dims, jnp.float32) * scale * level
    return jnp.minimum(jnp.maximum(values, -most), most).astype(kind)


def setup_inputs(seed: int = 0, part: int = 0) -> dict:
    splits = jax.random.split(jax.random.key(seed), 8)
    own_keys = jax.random.split(jax.random.fold_in(splits[7], part), 8)
    return {
        "hidden_in": draw_hidden_in(jax.random.fold_in(jax.random.fold_in(splits[7], part), 71), part),
        "norm_gain": jnp.clip(1.0 + 0.18 * jax.random.normal(splits[1], (D,), jnp.float32), 0.1, 1.9),
        "qkv_weight": normal_values(splits[2], (D, COLS), D ** -0.5, 0.046875, ((0, 2), (1, 8))),
        "out_weight": normal_values(splits[3], (QH * HD, D), (QH * HD // 16) ** -0.5, 0.25, ((0, 2), (1, 8))),
        "cache_keys": draw_cache_keys(jax.random.fold_in(jax.random.fold_in(splits[7], part), 71), part),
        "cache_values": normal_values(own_keys[5], (ROWS, CTX, KVH * HD), 1.0, 6.0, ((0, 8), (2, 2))),
        "cache_lengths": draw_cache_lengths(jax.random.fold_in(jax.random.fold_in(splits[7], part), 71), part),
    }


rope_theta = 500000.0
norm_eps = 1e-05

def rotary(values, position):
    half = values.shape[-1] // 2
    frequency = rope_theta ** (-jnp.arange(half, dtype=jnp.float32) * 2.0 / values.shape[-1])
    angles = position[..., None] * frequency
    cosine = jnp.cos(angles)
    sine = jnp.sin(angles)
    first = values[..., :half]
    second = values[..., half:]
    return jnp.concatenate([first * cosine - second * sine, second * cosine + first * sine], -1)

def attend_row(joined, keys, values, length):
    groups = joined.shape[0]
    share = joined.shape[1] - 2
    head_dim = joined.shape[2]
    position = length.astype(jnp.float32)
    query = (rotary(joined[:, :share], position) * head_dim ** (-0.5)).astype(jnp.bfloat16)
    new_key = rotary(joined[:, share], position).astype(jnp.bfloat16)
    new_value = joined[:, share + 1].astype(jnp.bfloat16)
    keys_four = keys.reshape(keys.shape[0], groups, head_dim).astype(jnp.float32)
    values_four = values.reshape(values.shape[0], groups, head_dim).astype(jnp.float32)
    scores = jnp.einsum('gjd,tgd->gjt', query.astype(jnp.float32), keys_four)
    own = lax.optimization_barrier(jnp.sum(query.astype(jnp.float32) * new_key.astype(jnp.float32)[:, None, :], -1))
    live = jnp.arange(keys.shape[0])[None, None, :] < length
    scores = jnp.where(live, scores, -1e+30)
    top = jnp.maximum(lax.optimization_barrier(jnp.max(scores, -1)), own)
    expo = jnp.exp(scores - top[..., None])
    own_expo = jnp.exp(own - top)
    total = lax.optimization_barrier(jnp.sum(expo, -1)) + own_expo
    probs = (expo / total[..., None]).astype(jnp.bfloat16)
    mixed = jnp.einsum('gjt,tgd->gjd', probs.astype(jnp.float32), values_four)
    mixed = mixed + (own_expo / total)[..., None] * new_value.astype(jnp.float32)[:, None, :]
    return mixed.astype(jnp.bfloat16).reshape(-1)

def reference(hidden_in, norm_gain, qkv_weight, out_weight, cache_keys, cache_values, cache_lengths):
    inputs = hidden_in.astype(jnp.float32)
    squares = lax.optimization_barrier(jnp.sum(inputs * inputs, -1))
    normed = (inputs * lax.rsqrt(squares / D + norm_eps)[:, None] * norm_gain).astype(jnp.bfloat16)
    joined = jnp.dot(normed, qkv_weight, preferred_element_type=jnp.float32)
    joined = joined.reshape(ROWS, KVH, GQ + 2, HD)

    def one_row(packed):
        return attend_row(packed[0], packed[1], packed[2], packed[3])
    mixed = lax.map(one_row, (joined, cache_keys, cache_values, cache_lengths))
    added = jnp.dot(mixed, out_weight, preferred_element_type=jnp.float32)
    return inputs + added
```

```python
import jax
import jax.numpy as jnp
from jax import lax
from jax.experimental import pallas as pl
from jax.experimental.pallas import tpu as pltpu
from jax.sharding import PartitionSpec as P

D = 16384
HD = 128
LANES = 128

rope_theta = 500000.0
norm_eps = 1e-05


def rotary(values, position):
    half = values.shape[-1] // 2
    frequency = rope_theta ** (-jnp.arange(half, dtype=jnp.float32) * 2.0 / values.shape[-1])
    angles = position[..., None] * frequency
    cosine = jnp.cos(angles)
    sine = jnp.sin(angles)
    first = values[..., :half]
    second = values[..., half:]
    return jnp.concatenate([first * cosine - second * sine, second * cosine + first * sine], -1)


def attend(joined, keys, values, lengths):
    count = joined.shape[0]
    groups = joined.shape[1]
    share = joined.shape[2] - 2
    head_dim = joined.shape[3]
    capacity = keys.shape[1]
    position = lengths.astype(jnp.float32)
    query = (rotary(joined[:, :, :share], position[:, None, None]) * head_dim ** (-0.5)).astype(
        jnp.bfloat16
    )
    new_key = rotary(joined[:, :, share], position[:, None]).astype(jnp.bfloat16)
    new_value = joined[:, :, share + 1].astype(jnp.bfloat16)
    keys_four = keys.reshape(count, capacity, groups, head_dim)
    values_four = values.reshape(count, capacity, groups, head_dim)
    scores = jnp.einsum("bgjd,btgd->bgjt", query, keys_four, preferred_element_type=jnp.float32)
    own = jnp.sum(query.astype(jnp.float32) * new_key.astype(jnp.float32)[:, :, None, :], -1)
    live = jnp.arange(capacity)[None, None, None, :] < lengths[:, None, None, None]
    scores = jnp.where(live, scores, -1e30)
    top = jnp.maximum(jnp.max(scores, -1), own)
    expo = jnp.exp(scores - top[..., None])
    own_expo = jnp.exp(own - top)
    total = jnp.sum(expo, -1) + own_expo
    probs = (expo / total[..., None]).astype(jnp.bfloat16)
    mixed = jnp.einsum("bgjt,btgd->bgjd", probs, values_four, preferred_element_type=jnp.float32)
    mixed = mixed + (own_expo / total)[..., None] * new_value.astype(jnp.float32)[:, :, None, :]
    return mixed.astype(jnp.bfloat16).reshape(count, groups * share * head_dim)


def head_kernel(x_ref, g_ref, o_ref, s_ref):
    x = x_ref[...].astype(jnp.float32)
    squares = x * x
    s_ref[...] = jnp.sum(squares.reshape(-1, 8, LANES), axis=0)
    scaled = (x * g_ref[...]).astype(jnp.bfloat16)
    for j in range(o_ref.shape[0]):
        o_ref[j] = scaled


def head(x, gain, copies):
    tiles = x.shape[0]
    return pl.pallas_call(
        head_kernel,
        out_shape=(
            jax.ShapeDtypeStruct((copies, tiles, LANES), jnp.bfloat16),
            jax.ShapeDtypeStruct((8, LANES), jnp.float32),
        ),
        compiler_params=pltpu.CompilerParams(vmem_limit_bytes=8 << 20),
        cost_estimate=pl.CostEstimate(flops=40_000_000_000, bytes_accessed=100_000_000, transcendentals=0),
    )(x, gain)


def product_kernel(x_ref, w_ref, o_ref):
    o_ref[...] = jnp.dot(x_ref[...], w_ref[...], preferred_element_type=jnp.float32)


def product(x, w):
    rows, depth = x.shape
    cols = w.shape[1]
    return pl.pallas_call(
        product_kernel,
        out_shape=jax.ShapeDtypeStruct((rows, cols), jnp.float32),
        compiler_params=pltpu.CompilerParams(vmem_limit_bytes=8 << 20),
        cost_estimate=pl.CostEstimate(flops=40_000_000_000, bytes_accessed=100_000_000, transcendentals=0),
    )(x, w)


def swap(x):
    return lax.ppermute(x, "narrow", [(0, 1), (1, 0)])


def collect(partial, core):
    rows, cols = partial.shape
    moved = lax.all_to_all(partial.reshape(rows, 1, cols), "wide", split_axis=0, concat_axis=0, tiled=True)
    half = rows // 2
    own = lax.dynamic_slice_in_dim(moved, core * half, half, 0)
    other = lax.dynamic_slice_in_dim(moved, (1 - core) * half, half, 0)
    return own + swap(other)


def body(hidden_in, norm_gain, qkv_weight, out_weight, cache_keys, cache_values, cache_lengths):
    wide = lax.axis_size("wide")
    core = lax.axis_index("narrow")
    feats = hidden_in.shape[1]
    tiles = feats // LANES
    scaled, squares = head(hidden_in.reshape(tiles, LANES), norm_gain.reshape(tiles, LANES), wide)
    squares = squares + swap(squares)
    scale = lax.rsqrt(jnp.sum(squares) / D + norm_eps)
    gathered = lax.all_to_all(scaled, "wide", split_axis=0, concat_axis=0, tiled=True)
    partial_qkv = product(gathered.reshape(wide, feats), qkv_weight)
    owned = collect(partial_qkv, core) * scale
    groups = cache_keys.shape[2] // HD
    owned = owned.reshape(1, groups, -1, HD)
    mixed = attend(owned, cache_keys, cache_values, cache_lengths)
    depth = mixed.shape[1]
    mixed = jnp.broadcast_to(mixed.reshape(1, depth // LANES, LANES), (wide, depth // LANES, LANES))
    spread = lax.all_to_all(mixed, "wide", split_axis=0, concat_axis=0, tiled=True)
    partial_out = product(spread.reshape(wide, depth), out_weight)
    added = collect(partial_out, core).reshape(1, -1)
    return hidden_in.astype(jnp.float32) + added


def solution(mesh):
    placed = (
        P(("group", "wide"), "narrow"),
        P("narrow"),
        P("narrow", "wide"),
        P("narrow", "wide"),
        P(("group", "wide"), None, "narrow"),
        P(("group", "wide"), None, "narrow"),
        P(("group", "wide")),
    )
    return jax.shard_map(
        body, mesh=mesh, in_specs=placed, out_specs=P(("group", "wide"), "narrow"), check_vma=False
    )
```

```python
import functools

import jax
import jax.numpy as jnp
from jax import lax
from jax.experimental import pallas as pl
from jax.experimental.pallas import tpu as pltpu
from jax.sharding import PartitionSpec as P

D = 16384
HD = 128
LANES = 128

rope_theta = 500000.0
norm_eps = 1e-05

VMEM = pl.BlockSpec(memory_space=pltpu.VMEM)
SMEM = pl.BlockSpec(memory_space=pltpu.SMEM)
HBM = pl.BlockSpec(memory_space=pl.ANY)


def params(limit):
    return pltpu.CompilerParams(vmem_limit_bytes=limit)


def cost(flops, size):
    return pl.CostEstimate(flops=flops, bytes_accessed=size, transcendentals=0)


def rope_tables(lengths):
    half = HD // 2
    frequency = rope_theta ** (-jnp.arange(half, dtype=jnp.float32) * 2.0 / HD)
    angles = lengths.astype(jnp.float32) * frequency
    cosine = jnp.cos(angles)
    sine = jnp.sin(angles)
    return jnp.stack([jnp.concatenate([cosine, cosine]), jnp.concatenate([-sine, sine])])


def square_kernel(x_ref, f_ref, s_ref):
    tiles = f_ref.shape[0]
    for j in range(tiles):
        f_ref[j : j + 1, :] = x_ref[:, j * LANES : (j + 1) * LANES].astype(jnp.float32)
    values = f_ref[...]
    s_ref[...] = jnp.sum((values * values).reshape(-1, 8, LANES), axis=0)


def norm_kernel(f_ref, g_ref, own_ref, other_ref, o_ref):
    total = jnp.sum(own_ref[...] + other_ref[...], keepdims=True)
    scale = lax.rsqrt(total / D + norm_eps)
    normed = (f_ref[...] * scale * g_ref[...]).astype(jnp.bfloat16)
    for j in range(o_ref.shape[0]):
        o_ref[j] = normed


def product_kernel(x_ref, w_ref, o_ref):
    result = jnp.dot(x_ref[...], w_ref[...], preferred_element_type=jnp.float32)
    for r in range(result.shape[0]):
        o_ref[r] = result[r : r + 1, :]


def product(x, w):
    rows, depth = x.shape
    cols = w.shape[1]
    return pl.pallas_call(
        product_kernel,
        out_shape=jax.ShapeDtypeStruct((rows, 1, cols), jnp.float32),
        in_specs=[VMEM, VMEM],
        out_specs=VMEM,
        compiler_params=params(4 << 20),
        cost_estimate=cost(2 * rows * depth * cols, w.size * 2),
    )(x, w)


def turn(values, table):
    half = values.shape[-1] // 2
    swapped = pltpu.roll(values, half, 1)
    return values * table[0:1, :] + swapped * table[1:2, :]


def attend_kernel(joined_ref, length, table, k_ref, v_ref, o_ref):
    groups, slots, head_dim = joined_ref.shape
    share = slots - 2
    capacity = k_ref.shape[0]
    live = lax.broadcasted_iota(jnp.int32, (share, capacity), 1) < length
    for g in range(groups):
        lanes = slice(g * head_dim, (g + 1) * head_dim)
        query = (turn(joined_ref[g, :share, :], table) * head_dim ** (-0.5)).astype(jnp.bfloat16)
        new_key = turn(joined_ref[g, share : share + 1, :], table).astype(jnp.bfloat16)
        new_value = joined_ref[g, share + 1 : share + 2, :].astype(jnp.bfloat16).astype(jnp.float32)
        scores = lax.dot_general(
            query, k_ref[:, lanes], (((1,), (1,)), ((), ())), preferred_element_type=jnp.float32
        )
        own = jnp.sum(query.astype(jnp.float32) * new_key.astype(jnp.float32), -1, keepdims=True)
        scores = jnp.where(live, scores, -1e30)
        top = jnp.maximum(jnp.max(scores, -1, keepdims=True), own)
        expo = jnp.exp(scores - top)
        own_expo = jnp.exp(own - top)
        total = jnp.sum(expo, -1, keepdims=True) + own_expo
        probs = (expo / total).astype(jnp.bfloat16)
        mixed = jnp.dot(probs, v_ref[:, lanes], preferred_element_type=jnp.float32)
        mixed = (mixed + (own_expo / total) * new_value).astype(jnp.bfloat16)
        for j in range(o_ref.shape[0]):
            o_ref[j, g * share : (g + 1) * share, :] = mixed


def direct_kernel(core_ref, len_ref, own_ref, other_ref, table_ref, k_ref, v_ref, o_ref, joined):
    half = own_ref.shape[0] // 2
    cols = own_ref.shape[2]
    groups, slots, _ = joined.shape
    first = core_ref[0] * half
    for b in range(half):
        for c in range(cols // LANES):
            piece = b * (cols // LANES) + c
            lanes = slice(c * LANES, (c + 1) * LANES)
            joined[piece // slots, piece % slots : piece % slots + 1, :] = (
                own_ref[first + b, :, lanes] + other_ref[first + b, :, lanes]
            )
    attend_kernel(joined, len_ref[0], table_ref[...], k_ref, v_ref, o_ref)


def given_kernel(len_ref, joined_ref, table_ref, k_ref, v_ref, o_ref):
    attend_kernel(joined_ref, len_ref[0], table_ref[...], k_ref, v_ref, o_ref)


def add_kernel(core_ref, x_ref, own_ref, other_ref, o_ref):
    half = own_ref.shape[0] // 2
    cols = own_ref.shape[2]
    first = core_ref[0] * half
    for b in range(half):
        lanes = slice(b * cols, (b + 1) * cols)
        added = own_ref[first + b] + other_ref[first + b]
        o_ref[:, lanes] = x_ref[:, lanes].astype(jnp.float32) + added


def swap(x):
    return lax.ppermute(x, "narrow", [(0, 1), (1, 0)])


def exchange(x):
    return lax.all_to_all(x, "wide", split_axis=0, concat_axis=0, tiled=True)


def body(hidden_in, norm_gain, qkv_weight, out_weight, cache_keys, cache_values, cache_lengths):
    wide = lax.axis_size("wide")
    core = lax.axis_index("narrow").astype(jnp.int32).reshape(1)
    table = rope_tables(cache_lengths)
    lengths = cache_lengths
    hidden_in, core, table, lengths = lax.optimization_barrier((hidden_in, core, table, lengths))
    feats = hidden_in.shape[1]
    tiles = feats // LANES
    values, squares = pl.pallas_call(
        square_kernel,
        out_shape=(
            jax.ShapeDtypeStruct((tiles, LANES), jnp.float32),
            jax.ShapeDtypeStruct((8, LANES), jnp.float32),
        ),
        in_specs=[VMEM],
        out_specs=(VMEM, VMEM),
        compiler_params=params(4 << 20),
        cost_estimate=cost(1000, 64_000),
    )(hidden_in)
    normed = pl.pallas_call(
        norm_kernel,
        out_shape=jax.ShapeDtypeStruct((wide, tiles, LANES), jnp.bfloat16),
        in_specs=[VMEM] * 4,
        out_specs=VMEM,
        compiler_params=params(4 << 20),
        cost_estimate=cost(1000, 40_000_000),
    )(values, norm_gain.reshape(tiles, LANES), squares, swap(squares))
    gathered = exchange(normed)
    partial_qkv = product(gathered.reshape(wide, feats), qkv_weight)
    moved = exchange(partial_qkv)
    other = swap(moved)
    capacity = cache_keys.shape[1]
    groups = cache_keys.shape[2] // HD
    keys = cache_keys.reshape(capacity, groups * HD)
    cached = cache_values.reshape(capacity, groups * HD)
    block = moved.shape[2]
    slots = wide // 2 * block // (groups * HD)
    share = slots - 2
    depth = groups * share * HD
    mixed_shape = jax.ShapeDtypeStruct((wide, depth // LANES, LANES), jnp.bfloat16)
    if block % LANES == 0:
        mixed = pl.pallas_call(
            direct_kernel,
            out_shape=mixed_shape,
            in_specs=[SMEM, SMEM, VMEM, VMEM, VMEM, VMEM, VMEM],
            out_specs=VMEM,
            scratch_shapes=[pltpu.VMEM((groups, slots, HD), jnp.float32)],
            compiler_params=params(4 << 20),
            cost_estimate=cost(1000, 40_000_000),
        )(core, lengths, moved, other, table, keys, cached)
    else:
        first = core[0] * (wide // 2)
        joined = lax.dynamic_slice_in_dim(moved + other, first, wide // 2, 0)
        mixed = pl.pallas_call(
            given_kernel,
            out_shape=mixed_shape,
            in_specs=[SMEM, VMEM, VMEM, VMEM, VMEM],
            out_specs=VMEM,
            compiler_params=params(4 << 20),
            cost_estimate=cost(1000, 40_000_000),
        )(lengths, joined.reshape(groups, slots, HD), table, keys, cached)
    spread = exchange(mixed)
    partial_out = product(spread.reshape(wide, depth), out_weight)
    added = exchange(partial_out)
    return pl.pallas_call(
        add_kernel,
        out_shape=jax.ShapeDtypeStruct((1, feats), jnp.float32),
        in_specs=[SMEM, VMEM, VMEM, VMEM],
        out_specs=VMEM,
        compiler_params=params(4 << 20),
        cost_estimate=cost(1000, 1_000_000),
    )(core, hidden_in, added, swap(added))


def solution(mesh):
    placed = (
        P(("group", "wide"), "narrow"),
        P("narrow"),
        P("narrow", "wide"),
        P("narrow", "wide"),
        P(("group", "wide"), None, "narrow"),
        P(("group", "wide"), None, "narrow"),
        P(("group", "wide")),
    )
    return jax.shard_map(
        body, mesh=mesh, in_specs=placed, out_specs=P(("group", "wide"), "narrow"), check_vma=False
    )
```

```python
import functools

import jax
import jax.numpy as jnp
from jax import lax
from jax.experimental import pallas as pl
from jax.experimental.pallas import tpu as pltpu
from jax.sharding import PartitionSpec as P

D = 16384
HD = 128
LANES = 128

rope_theta = 500000.0
norm_eps = 1e-05

VMEM = pl.BlockSpec(memory_space=pltpu.VMEM)
SMEM = pl.BlockSpec(memory_space=pltpu.SMEM)
HBM = pl.BlockSpec(memory_space=pl.ANY)


def params(limit):
    return pltpu.CompilerParams(vmem_limit_bytes=limit)


def cost(flops, size):
    return pl.CostEstimate(flops=flops, bytes_accessed=size, transcendentals=0)


def rope_tables(lengths):
    half = HD // 2
    frequency = rope_theta ** (-jnp.arange(half, dtype=jnp.float32) * 2.0 / HD)
    angles = lengths.astype(jnp.float32) * frequency
    cosine = jnp.cos(angles)
    sine = jnp.sin(angles)
    return jnp.stack([jnp.concatenate([cosine, cosine]), jnp.concatenate([-sine, sine])])


def square_kernel(x_ref, f_ref, s_ref):
    tiles = f_ref.shape[0]
    for j in range(tiles):
        f_ref[j : j + 1, :] = x_ref[:, j * LANES : (j + 1) * LANES].astype(jnp.float32)
    values = f_ref[...]
    s_ref[...] = jnp.sum((values * values).reshape(-1, 8, LANES), axis=0)


def norm_kernel(f_ref, g_ref, own_ref, other_ref, o_ref):
    total = jnp.sum(own_ref[...] + other_ref[...], keepdims=True)
    scale = lax.rsqrt(total / D + norm_eps)
    normed = (f_ref[...] * scale * g_ref[...]).astype(jnp.bfloat16)
    for j in range(o_ref.shape[0]):
        o_ref[j] = normed


def product_kernel(x_ref, w_ref, o_ref):
    result = jnp.dot(x_ref[...], w_ref[...], preferred_element_type=jnp.float32)
    for r in range(result.shape[0]):
        o_ref[r] = result[r : r + 1, :]


def product(x, w):
    rows, depth = x.shape
    cols = w.shape[1]
    return pl.pallas_call(
        product_kernel,
        out_shape=jax.ShapeDtypeStruct((rows, 1, cols), jnp.float32),
        in_specs=[VMEM, VMEM],
        out_specs=VMEM,
        compiler_params=params(4 << 20),
        cost_estimate=cost(2 * rows * depth * cols, w.size * 2),
    )(x, w)


def turn(values, table):
    half = values.shape[-1] // 2
    swapped = pltpu.roll(values, half, 1)
    return values * table[0:1, :] + swapped * table[1:2, :]


def attend_kernel(joined_ref, length, table, k_ref, v_ref, o_ref):
    groups, slots, head_dim = joined_ref.shape
    share = slots - 2
    capacity = k_ref.shape[0]
    live = lax.broadcasted_iota(jnp.int32, (share, capacity), 1) < length
    for g in range(groups):
        lanes = slice(g * head_dim, (g + 1) * head_dim)
        query = (turn(joined_ref[g, :share, :], table) * head_dim ** (-0.5)).astype(jnp.bfloat16)
        new_key = turn(joined_ref[g, share : share + 1, :], table).astype(jnp.bfloat16)
        new_value = joined_ref[g, share + 1 : share + 2, :].astype(jnp.bfloat16).astype(jnp.float32)
        scores = lax.dot_general(
            query, k_ref[:, lanes], (((1,), (1,)), ((), ())), preferred_element_type=jnp.float32
        )
        own = jnp.sum(query.astype(jnp.float32) * new_key.astype(jnp.float32), -1, keepdims=True)
        scores = jnp.where(live, scores, -1e30)
        top = jnp.maximum(jnp.max(scores, -1, keepdims=True), own)
        expo = jnp.exp(scores - top)
        own_expo = jnp.exp(own - top)
        total = jnp.sum(expo, -1, keepdims=True) + own_expo
        probs = (expo / total).astype(jnp.bfloat16)
        mixed = jnp.dot(probs, v_ref[:, lanes], preferred_element_type=jnp.float32)
        mixed = (mixed + (own_expo / total) * new_value).astype(jnp.bfloat16)
        for j in range(o_ref.shape[0]):
            o_ref[j, g * share : (g + 1) * share, :] = mixed


def direct_kernel(core_ref, len_ref, own_ref, other_ref, table_ref, k_ref, v_ref, o_ref, joined):
    half = own_ref.shape[0] // 2
    cols = own_ref.shape[2]
    groups, slots, _ = joined.shape
    first = core_ref[0] * half
    for b in range(half):
        for c in range(cols // LANES):
            piece = b * (cols // LANES) + c
            lanes = slice(c * LANES, (c + 1) * LANES)
            joined[piece // slots, piece % slots : piece % slots + 1, :] = (
                own_ref[first + b, :, lanes] + other_ref[first + b, :, lanes]
            )
    attend_kernel(joined, len_ref[0], table_ref[...], k_ref, v_ref, o_ref)


def given_kernel(len_ref, joined_ref, table_ref, k_ref, v_ref, o_ref):
    attend_kernel(joined_ref, len_ref[0], table_ref[...], k_ref, v_ref, o_ref)


def add_kernel(core_ref, x_ref, own_ref, other_ref, o_ref):
    half = own_ref.shape[0] // 2
    cols = own_ref.shape[2]
    first = core_ref[0] * half
    for b in range(half):
        lanes = slice(b * cols, (b + 1) * cols)
        added = own_ref[first + b] + other_ref[first + b]
        o_ref[:, lanes] = x_ref[:, lanes].astype(jnp.float32) + added


def swap(x):
    return lax.ppermute(x, "narrow", [(0, 1), (1, 0)])


def exchange(x):
    return lax.all_to_all(x, "wide", split_axis=0, concat_axis=0, tiled=True)


def body(hidden_in, norm_gain, qkv_weight, out_weight, cache_keys, cache_values, cache_lengths):
    wide = lax.axis_size("wide")
    core = lax.axis_index("narrow").astype(jnp.int32).reshape(1)
    table = rope_tables(cache_lengths)
    lengths = cache_lengths
    hidden_in, core, table, lengths = lax.optimization_barrier((hidden_in, core, table, lengths))
    feats = hidden_in.shape[1]
    tiles = feats // LANES
    values, squares = pl.pallas_call(
        square_kernel,
        out_shape=(
            jax.ShapeDtypeStruct((tiles, LANES), jnp.float32),
            jax.ShapeDtypeStruct((8, LANES), jnp.float32),
        ),
        in_specs=[VMEM],
        out_specs=(VMEM, VMEM),
        compiler_params=params(4 << 20),
        cost_estimate=cost(1000, 64_000),
    )(hidden_in)
    normed = pl.pallas_call(
        norm_kernel,
        out_shape=jax.ShapeDtypeStruct((wide, tiles, LANES), jnp.bfloat16),
        in_specs=[VMEM] * 4,
        out_specs=VMEM,
        compiler_params=params(4 << 20),
        cost_estimate=cost(40_000_000_000, 40_000_000),
    )(values, norm_gain.reshape(tiles, LANES), squares, swap(squares))
    gathered = exchange(normed)
    partial_qkv = product(gathered.reshape(wide, feats), qkv_weight)
    moved = exchange(partial_qkv)
    other = swap(moved)
    capacity = cache_keys.shape[1]
    groups = cache_keys.shape[2] // HD
    keys = cache_keys.reshape(capacity, groups * HD)
    cached = cache_values.reshape(capacity, groups * HD)
    block = moved.shape[2]
    slots = wide // 2 * block // (groups * HD)
    share = slots - 2
    depth = groups * share * HD
    mixed_shape = jax.ShapeDtypeStruct((wide, depth // LANES, LANES), jnp.bfloat16)
    if block % LANES == 0:
        mixed = pl.pallas_call(
            direct_kernel,
            out_shape=mixed_shape,
            in_specs=[SMEM, SMEM, VMEM, VMEM, VMEM, VMEM, VMEM],
            out_specs=VMEM,
            scratch_shapes=[pltpu.VMEM((groups, slots, HD), jnp.float32)],
            compiler_params=params(4 << 20),
            cost_estimate=cost(1000, 40_000_000),
        )(core, lengths, moved, other, table, keys, cached)
    else:
        first = core[0] * (wide // 2)
        joined = lax.dynamic_slice_in_dim(moved + other, first, wide // 2, 0)
        mixed = pl.pallas_call(
            given_kernel,
            out_shape=mixed_shape,
            in_specs=[SMEM, VMEM, VMEM, VMEM, VMEM],
            out_specs=VMEM,
            compiler_params=params(4 << 20),
            cost_estimate=cost(1000, 40_000_000),
        )(lengths, joined.reshape(groups, slots, HD), table, keys, cached)
    spread = exchange(mixed)
    partial_out = product(spread.reshape(wide, depth), out_weight)
    added = exchange(partial_out)
    return pl.pallas_call(
        add_kernel,
        out_shape=jax.ShapeDtypeStruct((1, feats), jnp.float32),
        in_specs=[SMEM, VMEM, VMEM, VMEM],
        out_specs=VMEM,
        compiler_params=params(4 << 20),
        cost_estimate=cost(1000, 1_000_000),
    )(core, hidden_in, added, swap(added))


def solution(mesh):
    placed = (
        P(("group", "wide"), "narrow"),
        P("narrow"),
        P("narrow", "wide"),
        P("narrow", "wide"),
        P(("group", "wide"), None, "narrow"),
        P(("group", "wide"), None, "narrow"),
        P(("group", "wide")),
    )
    return jax.shard_map(
        body, mesh=mesh, in_specs=placed, out_specs=P(("group", "wide"), "narrow"), check_vma=False
    )
```

```python
import functools

import jax
import jax.numpy as jnp
from jax import lax
from jax.experimental import pallas as pl
from jax.experimental.pallas import tpu as pltpu
from jax.sharding import PartitionSpec as P

D = 16384
HD = 128
LANES = 128

rope_theta = 500000.0
norm_eps = 1e-05

VMEM = pl.BlockSpec(memory_space=pltpu.VMEM)
SMEM = pl.BlockSpec(memory_space=pltpu.SMEM)
HBM = pl.BlockSpec(memory_space=pltpu.HBM)


def params(limit):
    return pltpu.CompilerParams(vmem_limit_bytes=limit)


def cost(flops, size):
    return pl.CostEstimate(flops=flops, bytes_accessed=size, transcendentals=0)


def rope_tables(lengths):
    half = HD // 2
    frequency = rope_theta ** (-jnp.arange(half, dtype=jnp.float32) * 2.0 / HD)
    angles = lengths.astype(jnp.float32) * frequency
    cosine = jnp.cos(angles)
    sine = jnp.sin(angles)
    return jnp.stack([jnp.concatenate([cosine, cosine]), jnp.concatenate([-sine, sine])])


def square_kernel(x_hbm, g_hbm, f_ref, g_ref, s_ref, x_ref, sems):
    tiles = f_ref.shape[0]
    x_copy = pltpu.make_async_copy(x_hbm, x_ref, sems.at[0])
    g_copy = pltpu.make_async_copy(g_hbm, g_ref, sems.at[1])
    x_copy.start()
    g_copy.start()
    x_copy.wait()
    g_copy.wait()
    for j in range(tiles):
        f_ref[j : j + 1, :] = x_ref[:, j * LANES : (j + 1) * LANES].astype(jnp.float32)
    values = f_ref[...]
    s_ref[...] = jnp.sum((values * values).reshape(-1, 8, LANES), axis=0)


def norm_kernel(f_ref, g_ref, own_ref, other_ref, o_ref):
    total = jnp.sum(own_ref[...] + other_ref[...], keepdims=True)
    scale = lax.rsqrt(total / D + norm_eps)
    normed = (f_ref[...] * scale * g_ref[...]).astype(jnp.bfloat16)
    for j in range(o_ref.shape[0]):
        o_ref[j] = normed


def product_kernel(x_ref, w_ref, o_ref):
    result = jnp.dot(x_ref[...], w_ref[...], preferred_element_type=jnp.float32)
    copies = o_ref.shape[0] // result.shape[0]
    for r in range(o_ref.shape[0]):
        row = r // copies
        o_ref[r] = result[row : row + 1, :]


def product(x, w, copies):
    rows, depth = x.shape
    cols = w.shape[1]
    return pl.pallas_call(
        product_kernel,
        out_shape=jax.ShapeDtypeStruct((rows * copies, 1, cols), jnp.float32),
        in_specs=[VMEM, VMEM],
        out_specs=VMEM,
        compiler_params=params(4 << 20),
        cost_estimate=cost(2 * rows * depth * cols, w.size * 2),
    )(x, w)


def turn(values, table):
    half = values.shape[-1] // 2
    swapped = pltpu.roll(values, half, 1)
    return values * table[0:1, :] + swapped * table[1:2, :]


def attend_kernel(joined_ref, length, table, k_ref, v_ref, o_ref):
    groups, slots, head_dim = joined_ref.shape
    share = slots - 2
    capacity = k_ref.shape[0]
    live = lax.broadcasted_iota(jnp.int32, (share, capacity), 1) < length
    for g in range(groups):
        lanes = slice(g * head_dim, (g + 1) * head_dim)
        query = (turn(joined_ref[g, :share, :], table) * head_dim ** (-0.5)).astype(jnp.bfloat16)
        new_key = turn(joined_ref[g, share : share + 1, :], table).astype(jnp.bfloat16)
        new_value = joined_ref[g, share + 1 : share + 2, :].astype(jnp.bfloat16).astype(jnp.float32)
        scores = lax.dot_general(
            query, k_ref[:, lanes], (((1,), (1,)), ((), ())), preferred_element_type=jnp.float32
        )
        own = jnp.sum(query.astype(jnp.float32) * new_key.astype(jnp.float32), -1, keepdims=True)
        scores = jnp.where(live, scores, -1e30)
        top = jnp.maximum(jnp.max(scores, -1, keepdims=True), own)
        expo = jnp.exp(scores - top)
        own_expo = jnp.exp(own - top)
        total = jnp.sum(expo, -1, keepdims=True) + own_expo
        probs = (expo / total).astype(jnp.bfloat16)
        mixed = jnp.dot(probs, v_ref[:, lanes], preferred_element_type=jnp.float32)
        mixed = (mixed + (own_expo / total) * new_value).astype(jnp.bfloat16)
        for j in range(o_ref.shape[0]):
            o_ref[j, g * share : (g + 1) * share, :] = mixed


def direct_kernel(core_ref, len_ref, parts_ref, table_ref, k_ref, v_ref, o_ref, joined):
    half = parts_ref.shape[0] // 4
    cols = parts_ref.shape[2]
    groups, slots, _ = joined.shape
    first = core_ref[0] * half
    for b in range(half):
        for c in range(cols // LANES):
            piece = b * (cols // LANES) + c
            lanes = slice(c * LANES, (c + 1) * LANES)
            joined[piece // slots, piece % slots : piece % slots + 1, :] = (
                parts_ref[2 * (first + b), :, lanes] + parts_ref[2 * (first + b) + 1, :, lanes]
            )
    attend_kernel(joined, len_ref[0], table_ref[...], k_ref, v_ref, o_ref)


def given_kernel(len_ref, joined_ref, table_ref, k_ref, v_ref, o_ref):
    attend_kernel(joined_ref, len_ref[0], table_ref[...], k_ref, v_ref, o_ref)


def add_kernel(core_ref, x_ref, own_ref, other_ref, o_ref):
    half = own_ref.shape[0] // 2
    cols = own_ref.shape[2]
    first = core_ref[0] * half
    for b in range(half):
        lanes = slice(b * cols, (b + 1) * cols)
        added = own_ref[first + b] + other_ref[first + b]
        o_ref[:, lanes] = x_ref[:, lanes].astype(jnp.float32) + added


def swap(x):
    return lax.ppermute(x, "narrow", [(0, 1), (1, 0)])


def exchange(x, axes="wide"):
    return lax.all_to_all(x, axes, split_axis=0, concat_axis=0, tiled=True)


def body(hidden_in, norm_gain, qkv_weight, out_weight, cache_keys, cache_values, cache_lengths):
    wide = lax.axis_size("wide")
    core = lax.axis_index("narrow").astype(jnp.int32).reshape(1)
    hidden_in, core = lax.optimization_barrier((hidden_in, core))
    feats = hidden_in.shape[1]
    tiles = feats // LANES
    values, gain, squares = pl.pallas_call(
        square_kernel,
        out_shape=(
            jax.ShapeDtypeStruct((tiles, LANES), jnp.float32),
            jax.ShapeDtypeStruct((tiles, LANES), jnp.float32),
            jax.ShapeDtypeStruct((8, LANES), jnp.float32),
        ),
        in_specs=[HBM, HBM],
        out_specs=(VMEM, VMEM, VMEM),
        scratch_shapes=[pltpu.VMEM(hidden_in.shape, hidden_in.dtype), pltpu.SemaphoreType.DMA((2,))],
        compiler_params=params(4 << 20),
        cost_estimate=cost(1000, 64_000),
    )(hidden_in, norm_gain.reshape(tiles, LANES))
    squares, lengths = lax.optimization_barrier((squares, cache_lengths))
    table = rope_tables(lengths)
    others, table = lax.optimization_barrier((swap(squares), table))
    normed = pl.pallas_call(
        norm_kernel,
        out_shape=jax.ShapeDtypeStruct((wide, tiles, LANES), jnp.bfloat16),
        in_specs=[VMEM] * 4,
        out_specs=VMEM,
        compiler_params=params(4 << 20),
        cost_estimate=cost(40_000_000_000, 40_000_000),
    )(values, gain, squares, others)
    gathered = exchange(normed)
    partial_qkv = product(gathered.reshape(wide, feats), qkv_weight, 2)
    moved = exchange(partial_qkv, ("wide", "narrow"))
    capacity = cache_keys.shape[1]
    groups = cache_keys.shape[2] // HD
    keys = cache_keys.reshape(capacity, groups * HD)
    cached = cache_values.reshape(capacity, groups * HD)
    block = moved.shape[2]
    slots = wide // 2 * block // (groups * HD)
    share = slots - 2
    depth = groups * share * HD
    mixed_shape = jax.ShapeDtypeStruct((wide, depth // LANES, LANES), jnp.bfloat16)
    if block % LANES == 0:
        mixed = pl.pallas_call(
            direct_kernel,
            out_shape=mixed_shape,
            in_specs=[SMEM, SMEM, VMEM, VMEM, VMEM, VMEM],
            out_specs=VMEM,
            scratch_shapes=[pltpu.VMEM((groups, slots, HD), jnp.float32)],
            compiler_params=params(4 << 20),
            cost_estimate=cost(1000, 40_000_000),
        )(core, lengths, moved, table, keys, cached)
    else:
        first = core[0] * (wide // 2)
        joined = jnp.sum(moved.reshape(wide, 2, block), axis=1)
        joined = lax.dynamic_slice_in_dim(joined, first, wide // 2, 0)
        mixed = pl.pallas_call(
            given_kernel,
            out_shape=mixed_shape,
            in_specs=[SMEM, VMEM, VMEM, VMEM, VMEM],
            out_specs=VMEM,
            compiler_params=params(4 << 20),
            cost_estimate=cost(1000, 40_000_000),
        )(lengths, joined.reshape(groups, slots, HD), table, keys, cached)
    spread = exchange(mixed)
    partial_out = product(spread.reshape(wide, depth), out_weight, 1)
    added = exchange(partial_out)
    return pl.pallas_call(
        add_kernel,
        out_shape=jax.ShapeDtypeStruct((1, feats), jnp.float32),
        in_specs=[SMEM, VMEM, VMEM, VMEM],
        out_specs=VMEM,
        compiler_params=params(4 << 20),
        cost_estimate=cost(1000, 1_000_000),
    )(core, hidden_in, added, swap(added))


def solution(mesh):
    placed = (
        P(("group", "wide"), "narrow"),
        P("narrow"),
        P("narrow", "wide"),
        P("narrow", "wide"),
        P(("group", "wide"), None, "narrow"),
        P(("group", "wide"), None, "narrow"),
        P(("group", "wide")),
    )
    return jax.shard_map(
        body, mesh=mesh, in_specs=placed, out_specs=P(("group", "wide"), "narrow"), check_vma=False
    )
```

```python
import functools

import jax
import jax.numpy as jnp
from jax import lax
from jax.experimental import pallas as pl
from jax.experimental.pallas import tpu as pltpu
from jax.sharding import PartitionSpec as P

D = 16384
HD = 128
LANES = 128

rope_theta = 500000.0
norm_eps = 1e-05

VMEM = pl.BlockSpec(memory_space=pltpu.VMEM)
SMEM = pl.BlockSpec(memory_space=pltpu.SMEM)


def params(limit):
    return pltpu.CompilerParams(vmem_limit_bytes=limit)


def cost(flops, size):
    return pl.CostEstimate(flops=flops, bytes_accessed=size, transcendentals=0)


def rope_tables(lengths):
    half = HD // 2
    frequency = rope_theta ** (-jnp.arange(half, dtype=jnp.float32) * 2.0 / HD)
    angles = lengths.astype(jnp.float32) * frequency
    cosine = jnp.cos(angles)
    sine = jnp.sin(angles)
    return jnp.stack([jnp.concatenate([cosine, cosine]), jnp.concatenate([-sine, sine])])


def square_kernel(x_ref, f_ref, s_ref):
    tiles = f_ref.shape[0]
    for j in range(tiles):
        f_ref[j : j + 1, :] = x_ref[:, j * LANES : (j + 1) * LANES].astype(jnp.float32)
    values = f_ref[...]
    s_ref[...] = jnp.sum((values * values).reshape(-1, 8, LANES), axis=0)


def norm_kernel(f_ref, g_ref, own_ref, other_ref, o_ref):
    total = jnp.sum(own_ref[...] + other_ref[...], keepdims=True)
    scale = lax.rsqrt(total / D + norm_eps)
    normed = (f_ref[...] * scale * g_ref[...]).astype(jnp.bfloat16)
    for j in range(o_ref.shape[0]):
        o_ref[j] = normed


def product_kernel(x_ref, w_ref, o_ref):
    result = jnp.dot(x_ref[...], w_ref[...], preferred_element_type=jnp.float32)
    rows = result.shape[0]
    lines, cols = o_ref.shape[1:]
    copies = o_ref.shape[0] // rows
    for r in range(rows):
        row = [result[r : r + 1, i * cols : (i + 1) * cols] for i in range(lines)]
        block = jnp.concatenate(row, axis=0).astype(o_ref.dtype)
        for j in range(copies):
            o_ref[r * copies + j] = block


def product(x, w, copies, lines, dtype):
    rows, depth = x.shape
    cols = w.shape[1]
    return pl.pallas_call(
        product_kernel,
        out_shape=jax.ShapeDtypeStruct((rows * copies, lines, cols // lines), dtype),
        in_specs=[VMEM, VMEM],
        out_specs=VMEM,
        compiler_params=params(4 << 20),
        cost_estimate=cost(2 * rows * depth * cols, w.size * 2),
    )(x, w)


def turn(values, table):
    half = values.shape[-1] // 2
    swapped = pltpu.roll(values, half, 1)
    return values * table[0:1, :] + swapped * table[1:2, :]


def attend_kernel(joined_ref, length, table, k_ref, v_ref, o_ref):
    groups, slots, head_dim = joined_ref.shape
    share = slots - 2
    capacity = k_ref.shape[0]
    live = lax.broadcasted_iota(jnp.int32, (share, capacity), 1) < length
    for g in range(groups):
        lanes = slice(g * head_dim, (g + 1) * head_dim)
        query = (turn(joined_ref[g, :share, :], table) * head_dim ** (-0.5)).astype(jnp.bfloat16)
        new_key = turn(joined_ref[g, share : share + 1, :], table).astype(jnp.bfloat16)
        new_value = joined_ref[g, share + 1 : share + 2, :].astype(jnp.bfloat16).astype(jnp.float32)
        scores = lax.dot_general(
            query, k_ref[:, lanes], (((1,), (1,)), ((), ())), preferred_element_type=jnp.float32
        )
        own = jnp.sum(query.astype(jnp.float32) * new_key.astype(jnp.float32), -1, keepdims=True)
        scores = jnp.where(live, scores, -1e30)
        top = jnp.maximum(jnp.max(scores, -1, keepdims=True), own)
        expo = jnp.exp(scores - top)
        own_expo = jnp.exp(own - top)
        total = jnp.sum(expo, -1, keepdims=True) + own_expo
        probs = (expo / total).astype(jnp.bfloat16)
        mixed = jnp.dot(probs, v_ref[:, lanes], preferred_element_type=jnp.float32)
        mixed = (mixed + (own_expo / total) * new_value).astype(jnp.bfloat16)
        for j in range(o_ref.shape[0]):
            o_ref[j, g * share : (g + 1) * share, :] = mixed


def direct_kernel(core_ref, len_ref, parts_ref, table_ref, k_ref, v_ref, o_ref, joined):
    half = parts_ref.shape[0] // 4
    cols = parts_ref.shape[2]
    groups, slots, _ = joined.shape
    first = core_ref[0] * half
    for b in range(half):
        for c in range(cols // LANES):
            piece = b * (cols // LANES) + c
            lanes = slice(c * LANES, (c + 1) * LANES)
            joined[piece // slots, piece % slots : piece % slots + 1, :] = (
                parts_ref[2 * (first + b), :, lanes] + parts_ref[2 * (first + b) + 1, :, lanes]
            )
    attend_kernel(joined, len_ref[0], table_ref[...], k_ref, v_ref, o_ref)


def given_kernel(len_ref, joined_ref, table_ref, k_ref, v_ref, o_ref):
    attend_kernel(joined_ref, len_ref[0], table_ref[...], k_ref, v_ref, o_ref)


def add_kernel(core_ref, x_ref, parts_ref, o_ref):
    half = parts_ref.shape[0] // 4
    lines, cols = parts_ref.shape[1:]
    first = core_ref[0] * half
    for b in range(half):
        one = parts_ref[2 * (first + b)].astype(jnp.float32)
        added = one + parts_ref[2 * (first + b) + 1].astype(jnp.float32)
        for i in range(lines):
            lanes = slice((b * lines + i) * cols, (b * lines + i + 1) * cols)
            o_ref[:, lanes] = x_ref[:, lanes].astype(jnp.float32) + added[i : i + 1, :]


def swap(x):
    return lax.ppermute(x, "narrow", [(0, 1), (1, 0)])


def exchange(x, axes="wide"):
    return lax.all_to_all(x, axes, split_axis=0, concat_axis=0, tiled=True)


def body(hidden_in, norm_gain, qkv_weight, out_weight, cache_keys, cache_values, cache_lengths):
    wide = lax.axis_size("wide")
    core = lax.axis_index("narrow").astype(jnp.int32).reshape(1)
    hidden_in, core = lax.optimization_barrier((hidden_in, core))
    feats = hidden_in.shape[1]
    tiles = feats // LANES
    values, squares = pl.pallas_call(
        square_kernel,
        out_shape=(
            jax.ShapeDtypeStruct((tiles, LANES), jnp.float32),
            jax.ShapeDtypeStruct((8, LANES), jnp.float32),
        ),
        in_specs=[VMEM],
        out_specs=(VMEM, VMEM),
        compiler_params=params(4 << 20),
        cost_estimate=cost(40_000_000_000, 64_000),
    )(hidden_in)
    squares, lengths = lax.optimization_barrier((squares, cache_lengths))
    table = rope_tables(lengths)
    others, table = lax.optimization_barrier((swap(squares), table))
    normed = pl.pallas_call(
        norm_kernel,
        out_shape=jax.ShapeDtypeStruct((wide, tiles, LANES), jnp.bfloat16),
        in_specs=[VMEM] * 4,
        out_specs=VMEM,
        compiler_params=params(4 << 20),
        cost_estimate=cost(40_000_000_000, 40_000_000),
    )(values, norm_gain.reshape(tiles, LANES), squares, others)
    gathered = exchange(normed)
    partial_qkv = product(gathered.reshape(wide, feats), qkv_weight, 2, 1, jnp.float32)
    moved = exchange(partial_qkv, ("wide", "narrow"))
    capacity = cache_keys.shape[1]
    groups = cache_keys.shape[2] // HD
    keys = cache_keys.reshape(capacity, groups * HD)
    cached = cache_values.reshape(capacity, groups * HD)
    block = moved.shape[2]
    slots = wide // 2 * block // (groups * HD)
    share = slots - 2
    depth = groups * share * HD
    mixed_shape = jax.ShapeDtypeStruct((wide, depth // LANES, LANES), jnp.bfloat16)
    if block % LANES == 0:
        mixed = pl.pallas_call(
            direct_kernel,
            out_shape=mixed_shape,
            in_specs=[SMEM, SMEM, VMEM, VMEM, VMEM, VMEM],
            out_specs=VMEM,
            scratch_shapes=[pltpu.VMEM((groups, slots, HD), jnp.float32)],
            compiler_params=params(4 << 20),
            cost_estimate=cost(1000, 40_000_000),
        )(core, lengths, moved, table, keys, cached)
    else:
        first = core[0] * (wide // 2)
        joined = jnp.sum(moved.reshape(wide, 2, block), axis=1)
        joined = lax.dynamic_slice_in_dim(joined, first, wide // 2, 0)
        mixed = pl.pallas_call(
            given_kernel,
            out_shape=mixed_shape,
            in_specs=[SMEM, VMEM, VMEM, VMEM, VMEM],
            out_specs=VMEM,
            compiler_params=params(4 << 20),
            cost_estimate=cost(1000, 40_000_000),
        )(lengths, joined.reshape(groups, slots, HD), table, keys, cached)
    spread = exchange(mixed)
    lines = 2 if out_weight.shape[1] % (2 * LANES) == 0 else 1
    partial_out = product(spread.reshape(wide, depth), out_weight, 2, lines, jnp.bfloat16)
    parts = exchange(partial_out, ("wide", "narrow"))
    return pl.pallas_call(
        add_kernel,
        out_shape=jax.ShapeDtypeStruct((1, feats), jnp.float32),
        in_specs=[SMEM, VMEM, VMEM],
        out_specs=VMEM,
        compiler_params=params(4 << 20),
        cost_estimate=cost(1000, 1_000_000),
    )(core, hidden_in, parts)


def solution(mesh):
    placed = (
        P(("group", "wide"), "narrow"),
        P("narrow"),
        P("narrow", "wide"),
        P("narrow", "wide"),
        P(("group", "wide"), None, "narrow"),
        P(("group", "wide"), None, "narrow"),
        P(("group", "wide")),
    )
    return jax.shard_map(
        body, mesh=mesh, in_specs=placed, out_specs=P(("group", "wide"), "narrow"), check_vma=False
    )
```

```python
import math

import jax
import jax.numpy as jnp
from jax import lax
from jax.experimental import pallas as pl
from jax.experimental.pallas import tpu as pltpu
from jax.sharding import PartitionSpec as P

D = 16384
HD = 128
LANES = 128

rope_theta = 500000.0
norm_eps = 1e-05

VMEM = pl.BlockSpec(memory_space=pltpu.VMEM)
SMEM = pl.BlockSpec(memory_space=pltpu.SMEM)


def params(limit):
    return pltpu.CompilerParams(vmem_limit_bytes=limit)


def cost(flops, size):
    return pl.CostEstimate(flops=flops, bytes_accessed=size, transcendentals=0)


def table_kernel(len_ref, after_ref, t_ref):
    half = HD // 2
    lane = lax.broadcasted_iota(jnp.int32, (1, HD), 1)
    place = jnp.where(lane < half, lane, lane - half).astype(jnp.float32)
    frequency = jnp.exp(place * (-2.0 / HD * math.log(rope_theta)))
    length = len_ref[0].astype(jnp.float32)
    angles = length * frequency
    sine = jnp.sin(angles)
    t_ref[0:1, :] = jnp.cos(angles)
    t_ref[1:2, :] = jnp.where(lane < half, -sine, sine)
    t_ref[2:3, :] = jnp.full((1, HD), length)


def square_kernel(x_ref, f_ref, s_ref):
    tiles = f_ref.shape[0]
    for j in range(tiles):
        f_ref[j : j + 1, :] = x_ref[:, j * LANES : (j + 1) * LANES].astype(jnp.float32)
    values = f_ref[...]
    s_ref[...] = jnp.sum((values * values).reshape(-1, 8, LANES), axis=0)


def norm_kernel(f_ref, g_ref, own_ref, other_ref, o_ref):
    total = jnp.sum(own_ref[...] + other_ref[...], keepdims=True)
    scale = lax.rsqrt(total / D + norm_eps)
    normed = (f_ref[...] * scale * g_ref[...]).astype(jnp.bfloat16)
    for j in range(o_ref.shape[0]):
        o_ref[j] = normed


def product_kernel(x_ref, w_ref, o_ref):
    result = jnp.dot(x_ref[...], w_ref[...], preferred_element_type=jnp.float32)
    rows = result.shape[0]
    lines, cols = o_ref.shape[1:]
    copies = o_ref.shape[0] // rows
    for r in range(rows):
        row = [result[r : r + 1, i * cols : (i + 1) * cols] for i in range(lines)]
        block = jnp.concatenate(row, axis=0).astype(o_ref.dtype)
        for j in range(copies):
            o_ref[r * copies + j] = block


def product(x, w, copies, lines, dtype):
    rows, depth = x.shape
    cols = w.shape[1]
    return pl.pallas_call(
        product_kernel,
        out_shape=jax.ShapeDtypeStruct((rows * copies, lines, cols // lines), dtype),
        in_specs=[VMEM, VMEM],
        out_specs=VMEM,
        compiler_params=params(4 << 20),
        cost_estimate=cost(2 * rows * depth * cols, w.size * 2),
    )(x, w)


def turn(values, table):
    half = values.shape[-1] // 2
    swapped = pltpu.roll(values, half, 1)
    return values * table[0:1, :] + swapped * table[1:2, :]


def attend_kernel(joined_ref, table, k_ref, v_ref, o_ref):
    groups, slots, head_dim = joined_ref.shape
    share = slots - 2
    capacity = k_ref.shape[0]
    places = lax.broadcasted_iota(jnp.int32, (share, capacity), 1).astype(jnp.float32)
    live = places < table[2:3, 0:1]
    for g in range(groups):
        lanes = slice(g * head_dim, (g + 1) * head_dim)
        query = (turn(joined_ref[g, :share, :], table) * head_dim ** (-0.5)).astype(jnp.bfloat16)
        new_key = turn(joined_ref[g, share : share + 1, :], table).astype(jnp.bfloat16)
        new_value = joined_ref[g, share + 1 : share + 2, :].astype(jnp.bfloat16).astype(jnp.float32)
        scores = lax.dot_general(
            query, k_ref[:, lanes], (((1,), (1,)), ((), ())), preferred_element_type=jnp.float32
        )
        own = jnp.sum(query.astype(jnp.float32) * new_key.astype(jnp.float32), -1, keepdims=True)
        scores = jnp.where(live, scores, -1e30)
        top = jnp.maximum(jnp.max(scores, -1, keepdims=True), own)
        expo = jnp.exp(scores - top)
        own_expo = jnp.exp(own - top)
        total = jnp.sum(expo, -1, keepdims=True) + own_expo
        share_of = 1.0 / total
        probs = (expo * share_of).astype(jnp.bfloat16)
        mixed = jnp.dot(probs, v_ref[:, lanes], preferred_element_type=jnp.float32)
        mixed = (mixed + (own_expo * share_of) * new_value).astype(jnp.bfloat16)
        for j in range(o_ref.shape[0]):
            o_ref[j, g * share : (g + 1) * share, :] = mixed


def direct_kernel(parts_ref, table_ref, k_ref, v_ref, o_ref, joined):
    half = parts_ref.shape[0] // 4
    cols = parts_ref.shape[2]
    groups, slots, _ = joined.shape
    first = lax.axis_index("narrow") * half
    for b in range(half):
        for c in range(cols // LANES):
            piece = b * (cols // LANES) + c
            lanes = slice(c * LANES, (c + 1) * LANES)
            joined[piece // slots, piece % slots : piece % slots + 1, :] = (
                parts_ref[2 * (first + b), :, lanes] + parts_ref[2 * (first + b) + 1, :, lanes]
            )
    attend_kernel(joined, table_ref[...], k_ref, v_ref, o_ref)


def given_kernel(joined_ref, table_ref, k_ref, v_ref, o_ref):
    attend_kernel(joined_ref, table_ref[...], k_ref, v_ref, o_ref)


def add_kernel(x_ref, parts_ref, o_ref):
    half = parts_ref.shape[0] // 4
    lines, cols = parts_ref.shape[1:]
    first = lax.axis_index("narrow") * half
    for b in range(half):
        one = parts_ref[2 * (first + b)].astype(jnp.float32)
        added = one + parts_ref[2 * (first + b) + 1].astype(jnp.float32)
        for i in range(lines):
            lanes = slice((b * lines + i) * cols, (b * lines + i + 1) * cols)
            o_ref[:, lanes] = x_ref[:, lanes].astype(jnp.float32) + added[i : i + 1, :]


def swap(x):
    return lax.ppermute(x, "narrow", [(0, 1), (1, 0)])


def exchange(x, axes="wide"):
    return lax.all_to_all(x, axes, split_axis=0, concat_axis=0, tiled=True)


def body(hidden_in, norm_gain, qkv_weight, out_weight, cache_keys, cache_values, cache_lengths):
    wide = lax.axis_size("wide")
    feats = hidden_in.shape[1]
    tiles = feats // LANES
    values, squares = pl.pallas_call(
        square_kernel,
        out_shape=(
            jax.ShapeDtypeStruct((tiles, LANES), jnp.float32),
            jax.ShapeDtypeStruct((8, LANES), jnp.float32),
        ),
        in_specs=[VMEM],
        out_specs=(VMEM, VMEM),
        compiler_params=params(4 << 20),
        cost_estimate=cost(2_000_000_000, 64_000),
    )(hidden_in)
    table = pl.pallas_call(
        table_kernel,
        out_shape=jax.ShapeDtypeStruct((3, HD), jnp.float32),
        in_specs=[SMEM, VMEM],
        out_specs=VMEM,
        compiler_params=params(4 << 20),
        cost_estimate=cost(1000, 1000),
    )(cache_lengths, squares)
    others, table = lax.optimization_barrier((swap(squares), table))
    normed = pl.pallas_call(
        norm_kernel,
        out_shape=jax.ShapeDtypeStruct((wide, tiles, LANES), jnp.bfloat16),
        in_specs=[VMEM] * 4,
        out_specs=VMEM,
        compiler_params=params(4 << 20),
        cost_estimate=cost(40_000_000_000, 40_000_000),
    )(values, norm_gain.reshape(tiles, LANES), squares, others)
    gathered = exchange(normed)
    partial_qkv = product(gathered.reshape(wide, feats), qkv_weight, 2, 1, jnp.float32)
    moved = exchange(partial_qkv, ("wide", "narrow"))
    capacity = cache_keys.shape[1]
    groups = cache_keys.shape[2] // HD
    keys = cache_keys.reshape(capacity, groups * HD)
    cached = cache_values.reshape(capacity, groups * HD)
    block = moved.shape[2]
    slots = wide // 2 * block // (groups * HD)
    share = slots - 2
    depth = groups * share * HD
    mixed_shape = jax.ShapeDtypeStruct((wide, depth // LANES, LANES), jnp.bfloat16)
    if block % LANES == 0:
        mixed = pl.pallas_call(
            direct_kernel,
            out_shape=mixed_shape,
            in_specs=[VMEM, VMEM, VMEM, VMEM],
            out_specs=VMEM,
            scratch_shapes=[pltpu.VMEM((groups, slots, HD), jnp.float32)],
            compiler_params=params(4 << 20),
            cost_estimate=cost(1000, 40_000_000),
        )(moved, table, keys, cached)
    else:
        first = lax.axis_index("narrow") * (wide // 2)
        joined = jnp.sum(moved.reshape(wide, 2, block), axis=1)
        joined = lax.dynamic_slice_in_dim(joined, first, wide // 2, 0)
        mixed = pl.pallas_call(
            given_kernel,
            out_shape=mixed_shape,
            in_specs=[VMEM, VMEM, VMEM, VMEM],
            out_specs=VMEM,
            compiler_params=params(4 << 20),
            cost_estimate=cost(1000, 40_000_000),
        )(joined.reshape(groups, slots, HD), table, keys, cached)
    spread = exchange(mixed)
    lines = 2 if out_weight.shape[1] % (2 * LANES) == 0 else 1
    partial_out = product(spread.reshape(wide, depth), out_weight, 2, lines, jnp.bfloat16)
    parts = exchange(partial_out, ("wide", "narrow"))
    return pl.pallas_call(
        add_kernel,
        out_shape=jax.ShapeDtypeStruct((1, feats), jnp.float32),
        in_specs=[VMEM, VMEM],
        out_specs=VMEM,
        compiler_params=params(4 << 20),
        cost_estimate=cost(1000, 1_000_000),
    )(hidden_in, parts)


def solution(mesh):
    placed = (
        P(("group", "wide"), "narrow"),
        P("narrow"),
        P("narrow", "wide"),
        P("narrow", "wide"),
        P(("group", "wide"), None, "narrow"),
        P(("group", "wide"), None, "narrow"),
        P(("group", "wide")),
    )
    return jax.shard_map(
        body, mesh=mesh, in_specs=placed, out_specs=P(("group", "wide"), "narrow"), check_vma=False
    )
```

```python
import math

import jax
import jax.numpy as jnp
from jax import lax
from jax.experimental import pallas as pl
from jax.experimental.pallas import tpu as pltpu
from jax.sharding import PartitionSpec as P

D = 16384
HD = 128
LANES = 128

rope_theta = 500000.0
norm_eps = 1e-05

VMEM = pl.BlockSpec(memory_space=pltpu.VMEM)
SMEM = pl.BlockSpec(memory_space=pltpu.SMEM)


def params(limit):
    return pltpu.CompilerParams(vmem_limit_bytes=limit)


def cost(flops, size):
    return pl.CostEstimate(flops=flops, bytes_accessed=size, transcendentals=0)


def table_kernel(len_ref, after_ref, t_ref):
    half = HD // 2
    lane = lax.broadcasted_iota(jnp.int32, (1, HD), 1)
    place = jnp.where(lane < half, lane, lane - half).astype(jnp.float32)
    frequency = jnp.exp(place * (-2.0 / HD * math.log(rope_theta)))
    length = len_ref[0].astype(jnp.float32)
    angles = length * frequency
    sine = jnp.sin(angles)
    t_ref[0:1, :] = jnp.cos(angles)
    t_ref[1:2, :] = jnp.where(lane < half, -sine, sine)
    t_ref[2:3, :] = jnp.full((1, HD), length)


def square_kernel(x_ref, f_ref, s_ref):
    tiles = f_ref.shape[0]
    for j in range(tiles):
        f_ref[j : j + 1, :] = x_ref[:, j * LANES : (j + 1) * LANES].astype(jnp.float32)
    values = f_ref[...]
    s_ref[...] = jnp.sum((values * values).reshape(-1, 8, LANES), axis=0)


def norm_kernel(f_ref, g_ref, own_ref, other_ref, o_ref):
    total = jnp.sum(own_ref[...] + other_ref[...], keepdims=True)
    scale = lax.rsqrt(total / D + norm_eps)
    normed = (f_ref[...] * scale * g_ref[...]).astype(jnp.bfloat16)
    for j in range(o_ref.shape[0]):
        o_ref[j] = normed


def product_kernel(x_ref, w_ref, o_ref):
    result = jnp.dot(x_ref[...], w_ref[...], preferred_element_type=jnp.float32)
    rows = result.shape[0]
    lines, cols = o_ref.shape[1:]
    copies = o_ref.shape[0] // rows
    for r in range(rows):
        row = [result[r : r + 1, i * cols : (i + 1) * cols] for i in range(lines)]
        block = jnp.concatenate(row, axis=0).astype(o_ref.dtype)
        for j in range(copies):
            o_ref[r * copies + j] = block


def product(x, w, copies, lines, dtype):
    rows, depth = x.shape
    cols = w.shape[1]
    return pl.pallas_call(
        product_kernel,
        out_shape=jax.ShapeDtypeStruct((rows * copies, lines, cols // lines), dtype),
        in_specs=[VMEM, VMEM],
        out_specs=VMEM,
        compiler_params=params(4 << 20),
        cost_estimate=cost(2 * rows * depth * cols, w.size * 2),
    )(x, w)


def turn(values, table):
    half = values.shape[-1] // 2
    swapped = pltpu.roll(values, half, 1)
    return values * table[0:1, :] + swapped * table[1:2, :]


def attend_kernel(joined_ref, table, k_ref, v_ref, o_ref):
    groups, slots, head_dim = joined_ref.shape
    share = slots - 2
    capacity = k_ref.shape[0]
    places = lax.broadcasted_iota(jnp.int32, (share, capacity), 1).astype(jnp.float32)
    live = places < table[2:3, 0:1]
    for g in range(groups):
        lanes = slice(g * head_dim, (g + 1) * head_dim)
        query = (turn(joined_ref[g, :share, :], table) * head_dim ** (-0.5)).astype(jnp.bfloat16)
        new_key = turn(joined_ref[g, share : share + 1, :], table).astype(jnp.bfloat16)
        new_value = joined_ref[g, share + 1 : share + 2, :].astype(jnp.bfloat16).astype(jnp.float32)
        scores = lax.dot_general(
            query, k_ref[:, lanes], (((1,), (1,)), ((), ())), preferred_element_type=jnp.float32
        )
        own = jnp.sum(query.astype(jnp.float32) * new_key.astype(jnp.float32), -1, keepdims=True)
        scores = jnp.where(live, scores, -1e30)
        top = jnp.maximum(jnp.max(scores, -1, keepdims=True), own)
        expo = jnp.exp(scores - top)
        own_expo = jnp.exp(own - top)
        total = jnp.sum(expo, -1, keepdims=True) + own_expo
        share_of = 1.0 / total
        probs = (expo * share_of).astype(jnp.bfloat16)
        mixed = jnp.dot(probs, v_ref[:, lanes], preferred_element_type=jnp.float32)
        mixed = (mixed + (own_expo * share_of) * new_value).astype(jnp.bfloat16)
        for j in range(o_ref.shape[0]):
            o_ref[j, g * share : (g + 1) * share, :] = mixed


def direct_kernel(parts_ref, table_ref, k_ref, v_ref, o_ref, joined):
    half = parts_ref.shape[0] // 4
    cols = parts_ref.shape[2]
    groups, slots, _ = joined.shape
    first = lax.axis_index("narrow") * half
    for b in range(half):
        for c in range(cols // LANES):
            piece = b * (cols // LANES) + c
            lanes = slice(c * LANES, (c + 1) * LANES)
            joined[piece // slots, piece % slots : piece % slots + 1, :] = (
                parts_ref[2 * (first + b), :, lanes] + parts_ref[2 * (first + b) + 1, :, lanes]
            )
    attend_kernel(joined, table_ref[...], k_ref, v_ref, o_ref)


def given_kernel(joined_ref, table_ref, k_ref, v_ref, o_ref):
    attend_kernel(joined_ref, table_ref[...], k_ref, v_ref, o_ref)


def add_kernel(x_ref, parts_ref, o_ref):
    half = parts_ref.shape[0] // 4
    lines, cols = parts_ref.shape[1:]
    first = lax.axis_index("narrow") * half
    for b in range(half):
        one = parts_ref[2 * (first + b)].astype(jnp.float32)
        added = one + parts_ref[2 * (first + b) + 1].astype(jnp.float32)
        for i in range(lines):
            lanes = slice((b * lines + i) * cols, (b * lines + i + 1) * cols)
            o_ref[:, lanes] = x_ref[:, lanes].astype(jnp.float32) + added[i : i + 1, :]


def swap(x):
    return lax.ppermute(x, "narrow", [(0, 1), (1, 0)])


def exchange(x, axes="wide"):
    return lax.all_to_all(x, axes, split_axis=0, concat_axis=0, tiled=True)


def body(hidden_in, norm_gain, qkv_weight, out_weight, cache_keys, cache_values, cache_lengths):
    wide = lax.axis_size("wide")
    feats = hidden_in.shape[1]
    tiles = feats // LANES
    values, squares = pl.pallas_call(
        square_kernel,
        out_shape=(
            jax.ShapeDtypeStruct((tiles, LANES), jnp.float32),
            jax.ShapeDtypeStruct((8, LANES), jnp.float32),
        ),
        in_specs=[VMEM],
        out_specs=(VMEM, VMEM),
        compiler_params=params(4 << 20),
        cost_estimate=cost(8_000_000_000, 64_000),
    )(hidden_in)
    table = pl.pallas_call(
        table_kernel,
        out_shape=jax.ShapeDtypeStruct((3, HD), jnp.float32),
        in_specs=[SMEM, VMEM],
        out_specs=VMEM,
        compiler_params=params(4 << 20),
        cost_estimate=cost(1000, 1000),
    )(cache_lengths, squares)
    others, table = lax.optimization_barrier((swap(squares), table))
    normed = pl.pallas_call(
        norm_kernel,
        out_shape=jax.ShapeDtypeStruct((wide, tiles, LANES), jnp.bfloat16),
        in_specs=[VMEM] * 4,
        out_specs=VMEM,
        compiler_params=params(4 << 20),
        cost_estimate=cost(200_000_000_000, 40_000_000),
    )(values, norm_gain.reshape(tiles, LANES), squares, others)
    gathered = exchange(normed)
    partial_qkv = product(gathered.reshape(wide, feats), qkv_weight, 2, 1, jnp.float32)
    moved = exchange(partial_qkv, ("wide", "narrow"))
    capacity = cache_keys.shape[1]
    groups = cache_keys.shape[2] // HD
    keys = cache_keys.reshape(capacity, groups * HD)
    cached = cache_values.reshape(capacity, groups * HD)
    block = moved.shape[2]
    slots = wide // 2 * block // (groups * HD)
    share = slots - 2
    depth = groups * share * HD
    mixed_shape = jax.ShapeDtypeStruct((wide, depth // LANES, LANES), jnp.bfloat16)
    if block % LANES == 0:
        mixed = pl.pallas_call(
            direct_kernel,
            out_shape=mixed_shape,
            in_specs=[VMEM, VMEM, VMEM, VMEM],
            out_specs=VMEM,
            scratch_shapes=[pltpu.VMEM((groups, slots, HD), jnp.float32)],
            compiler_params=params(4 << 20),
            cost_estimate=cost(1000, 40_000_000),
        )(moved, table, keys, cached)
    else:
        first = lax.axis_index("narrow") * (wide // 2)
        joined = jnp.sum(moved.reshape(wide, 2, block), axis=1)
        joined = lax.dynamic_slice_in_dim(joined, first, wide // 2, 0)
        mixed = pl.pallas_call(
            given_kernel,
            out_shape=mixed_shape,
            in_specs=[VMEM, VMEM, VMEM, VMEM],
            out_specs=VMEM,
            compiler_params=params(4 << 20),
            cost_estimate=cost(1000, 40_000_000),
        )(joined.reshape(groups, slots, HD), table, keys, cached)
    spread = exchange(mixed)
    lines = 2 if out_weight.shape[1] % (2 * LANES) == 0 else 1
    partial_out = product(spread.reshape(wide, depth), out_weight, 2, lines, jnp.bfloat16)
    parts = exchange(partial_out, ("wide", "narrow"))
    return pl.pallas_call(
        add_kernel,
        out_shape=jax.ShapeDtypeStruct((1, feats), jnp.float32),
        in_specs=[VMEM, VMEM],
        out_specs=VMEM,
        compiler_params=params(4 << 20),
        cost_estimate=cost(1000, 1_000_000),
    )(hidden_in, parts)


def solution(mesh):
    placed = (
        P(("group", "wide"), "narrow"),
        P("narrow"),
        P("narrow", "wide"),
        P("narrow", "wide"),
        P(("group", "wide"), None, "narrow"),
        P(("group", "wide"), None, "narrow"),
        P(("group", "wide")),
    )
    return jax.shard_map(
        body, mesh=mesh, in_specs=placed, out_specs=P(("group", "wide"), "narrow"), check_vma=False
    )
```

```python
import math

import jax
import jax.numpy as jnp
from jax import lax
from jax.experimental import pallas as pl
from jax.experimental.pallas import tpu as pltpu
from jax.sharding import PartitionSpec as P

D = 16384
HD = 128
LANES = 128

rope_theta = 500000.0
norm_eps = 1e-05

VMEM = pl.BlockSpec(memory_space=pltpu.VMEM)
SMEM = pl.BlockSpec(memory_space=pltpu.SMEM)


def params(limit):
    return pltpu.CompilerParams(vmem_limit_bytes=limit)


def cost(flops, size):
    return pl.CostEstimate(flops=flops, bytes_accessed=size, transcendentals=0)


def table_kernel(len_ref, after_ref, t_ref):
    half = HD // 2
    lane = lax.broadcasted_iota(jnp.int32, (1, HD), 1)
    place = jnp.where(lane < half, lane, lane - half).astype(jnp.float32)
    frequency = jnp.exp(place * (-2.0 / HD * math.log(rope_theta)))
    length = len_ref[0].astype(jnp.float32)
    angles = length * frequency
    sine = jnp.sin(angles)
    t_ref[0:1, :] = jnp.cos(angles)
    t_ref[1:2, :] = jnp.where(lane < half, -sine, sine)
    t_ref[2:3, :] = jnp.full((1, HD), length)


def square_kernel(x_ref, f_ref, s_ref):
    tiles = f_ref.shape[0]
    for j in range(tiles):
        f_ref[j : j + 1, :] = x_ref[:, j * LANES : (j + 1) * LANES].astype(jnp.float32)
    values = f_ref[...]
    s_ref[...] = jnp.sum((values * values).reshape(-1, 8, LANES), axis=0)


def norm_kernel(f_ref, g_ref, own_ref, other_ref, o_ref):
    total = jnp.sum(own_ref[...] + other_ref[...], keepdims=True)
    scale = lax.rsqrt(total / D + norm_eps)
    normed = (f_ref[...] * scale * g_ref[...]).astype(jnp.bfloat16)
    for j in range(o_ref.shape[0]):
        o_ref[j] = normed


def product_kernel(x_ref, w_ref, o_ref):
    result = jnp.dot(x_ref[...], w_ref[...], preferred_element_type=jnp.float32)
    rows = result.shape[0]
    lines, cols = o_ref.shape[1:]
    copies = o_ref.shape[0] // rows
    for r in range(rows):
        row = [result[r : r + 1, i * cols : (i + 1) * cols] for i in range(lines)]
        block = jnp.concatenate(row, axis=0).astype(o_ref.dtype)
        for j in range(copies):
            o_ref[r * copies + j] = block


def product(x, w, copies, lines, dtype):
    rows, depth = x.shape
    cols = w.shape[1]
    return pl.pallas_call(
        product_kernel,
        out_shape=jax.ShapeDtypeStruct((rows * copies, lines, cols // lines), dtype),
        in_specs=[VMEM, VMEM],
        out_specs=VMEM,
        compiler_params=params(4 << 20),
        cost_estimate=cost(2 * rows * depth * cols, w.size * 2),
    )(x, w)


def turn(values, table):
    half = values.shape[-1] // 2
    swapped = pltpu.roll(values, half, 1)
    return values * table[0:1, :] + swapped * table[1:2, :]


def attend_kernel(joined_ref, table, k_ref, v_ref, o_ref):
    groups, slots, head_dim = joined_ref.shape
    share = slots - 2
    capacity = k_ref.shape[0]
    places = lax.broadcasted_iota(jnp.int32, (share, capacity), 1).astype(jnp.float32)
    live = places < table[2:3, 0:1]
    for g in range(groups):
        lanes = slice(g * head_dim, (g + 1) * head_dim)
        query = (turn(joined_ref[g, :share, :], table) * head_dim ** (-0.5)).astype(jnp.bfloat16)
        new_key = turn(joined_ref[g, share : share + 1, :], table).astype(jnp.bfloat16)
        new_value = joined_ref[g, share + 1 : share + 2, :].astype(jnp.bfloat16).astype(jnp.float32)
        scores = lax.dot_general(
            query, k_ref[:, lanes], (((1,), (1,)), ((), ())), preferred_element_type=jnp.float32
        )
        own = jnp.sum(query.astype(jnp.float32) * new_key.astype(jnp.float32), -1, keepdims=True)
        scores = jnp.where(live, scores, -1e30)
        top = jnp.maximum(jnp.max(scores, -1, keepdims=True), own)
        expo = jnp.exp(scores - top)
        own_expo = jnp.exp(own - top)
        total = jnp.sum(expo, -1, keepdims=True) + own_expo
        share_of = 1.0 / total
        probs = (expo * share_of).astype(jnp.bfloat16)
        mixed = jnp.dot(probs, v_ref[:, lanes], preferred_element_type=jnp.float32)
        mixed = (mixed + (own_expo * share_of) * new_value).astype(jnp.bfloat16)
        for j in range(o_ref.shape[0]):
            o_ref[j, g * share : (g + 1) * share, :] = mixed


def direct_kernel(parts_ref, table_ref, k_ref, v_ref, o_ref, joined):
    half = parts_ref.shape[0] // 4
    cols = parts_ref.shape[2]
    groups, slots, _ = joined.shape
    first = lax.axis_index("narrow") * half
    for b in range(half):
        for c in range(cols // LANES):
            piece = b * (cols // LANES) + c
            lanes = slice(c * LANES, (c + 1) * LANES)
            joined[piece // slots, piece % slots : piece % slots + 1, :] = (
                parts_ref[2 * (first + b), :, lanes] + parts_ref[2 * (first + b) + 1, :, lanes]
            )
    attend_kernel(joined, table_ref[...], k_ref, v_ref, o_ref)


def given_kernel(joined_ref, table_ref, k_ref, v_ref, o_ref):
    attend_kernel(joined_ref, table_ref[...], k_ref, v_ref, o_ref)


def add_kernel(x_ref, parts_ref, o_ref):
    half = parts_ref.shape[0] // 4
    lines, cols = parts_ref.shape[1:]
    first = lax.axis_index("narrow") * half
    for b in range(half):
        one = parts_ref[2 * (first + b)].astype(jnp.float32)
        added = one + parts_ref[2 * (first + b) + 1].astype(jnp.float32)
        for i in range(lines):
            lanes = slice((b * lines + i) * cols, (b * lines + i + 1) * cols)
            o_ref[:, lanes] = x_ref[:, lanes].astype(jnp.float32) + added[i : i + 1, :]


def swap(x):
    return lax.ppermute(x, "narrow", [(0, 1), (1, 0)])


def exchange(x, axes="wide"):
    return lax.all_to_all(x, axes, split_axis=0, concat_axis=0, tiled=True)


def body(hidden_in, norm_gain, qkv_weight, out_weight, cache_keys, cache_values, cache_lengths):
    wide = lax.axis_size("wide")
    feats = hidden_in.shape[1]
    tiles = feats // LANES
    values, squares = pl.pallas_call(
        square_kernel,
        out_shape=(
            jax.ShapeDtypeStruct((tiles, LANES), jnp.float32),
            jax.ShapeDtypeStruct((8, LANES), jnp.float32),
        ),
        in_specs=[VMEM],
        out_specs=(VMEM, VMEM),
        compiler_params=params(4 << 20),
        cost_estimate=cost(8_000_000_000, 64_000),
    )(hidden_in)
    table = pl.pallas_call(
        table_kernel,
        out_shape=jax.ShapeDtypeStruct((3, HD), jnp.float32),
        in_specs=[SMEM, VMEM],
        out_specs=VMEM,
        compiler_params=params(4 << 20),
        cost_estimate=cost(1000, 1000),
    )(cache_lengths, squares)
    others, table = lax.optimization_barrier((swap(squares), table))
    normed = pl.pallas_call(
        norm_kernel,
        out_shape=jax.ShapeDtypeStruct((wide, tiles, LANES), jnp.bfloat16),
        in_specs=[VMEM] * 4,
        out_specs=VMEM,
        compiler_params=params(4 << 20),
        cost_estimate=cost(200_000_000_000, 40_000_000),
    )(values, norm_gain.reshape(tiles, LANES), squares, others)
    gathered = exchange(normed)
    partial_qkv = product(gathered.reshape(wide, feats), qkv_weight, 2, 1, jnp.float32)
    moved = exchange(partial_qkv, ("wide", "narrow"))
    capacity = cache_keys.shape[1]
    groups = cache_keys.shape[2] // HD
    keys = cache_keys.reshape(capacity, groups * HD)
    cached = cache_values.reshape(capacity, groups * HD)
    block = moved.shape[2]
    slots = wide // 2 * block // (groups * HD)
    share = slots - 2
    depth = groups * share * HD
    mixed_shape = jax.ShapeDtypeStruct((wide, depth // LANES, LANES), jnp.bfloat16)
    if block % LANES == 0:
        mixed = pl.pallas_call(
            direct_kernel,
            out_shape=mixed_shape,
            in_specs=[VMEM, VMEM, VMEM, VMEM],
            out_specs=VMEM,
            scratch_shapes=[pltpu.VMEM((groups, slots, HD), jnp.float32)],
            compiler_params=params(4 << 20),
            cost_estimate=cost(200_000_000_000, 40_000_000),
        )(moved, table, keys, cached)
    else:
        first = lax.axis_index("narrow") * (wide // 2)
        joined = jnp.sum(moved.reshape(wide, 2, block), axis=1)
        joined = lax.dynamic_slice_in_dim(joined, first, wide // 2, 0)
        mixed = pl.pallas_call(
            given_kernel,
            out_shape=mixed_shape,
            in_specs=[VMEM, VMEM, VMEM, VMEM],
            out_specs=VMEM,
            compiler_params=params(4 << 20),
            cost_estimate=cost(200_000_000_000, 40_000_000),
        )(joined.reshape(groups, slots, HD), table, keys, cached)
    spread = exchange(mixed)
    lines = 2 if out_weight.shape[1] % (2 * LANES) == 0 else 1
    partial_out = product(spread.reshape(wide, depth), out_weight, 2, lines, jnp.bfloat16)
    parts = exchange(partial_out, ("wide", "narrow"))
    return pl.pallas_call(
        add_kernel,
        out_shape=jax.ShapeDtypeStruct((1, feats), jnp.float32),
        in_specs=[VMEM, VMEM],
        out_specs=VMEM,
        compiler_params=params(4 << 20),
        cost_estimate=cost(1000, 1_000_000),
    )(hidden_in, parts)


def solution(mesh):
    placed = (
        P(("group", "wide"), "narrow"),
        P("narrow"),
        P("narrow", "wide"),
        P("narrow", "wide"),
        P(("group", "wide"), None, "narrow"),
        P(("group", "wide"), None, "narrow"),
        P(("group", "wide")),
    )
    return jax.shard_map(
        body, mesh=mesh, in_specs=placed, out_specs=P(("group", "wide"), "narrow"), check_vma=False
    )
```
